32 devices in a mesh: dp: 2 (over x), context: 4 (over y, core), tensor: 4 (over z).
Axes of the slice: x: 2, y: 2, z: 4, core: 2. Of those that a mesh axis runs over, the one named last changes fastest.
Arguments:
- hidden_in: bfloat16 [16, 1024, 576], P('dp', ('context', 'tensor')), may hold values from -6 to 6
- attn_gain: bfloat16 [576], P('dp'), may hold values from 0.099609375 to 1.8984375
- query_weight: bfloat16 [576, 576], P('dp'), may hold values from -0.25 to 0.25
- key_weight: bfloat16 [576, 192], P('dp'), may hold values from -0.25 to 0.25
- value_weight: bfloat16 [576, 192], P('dp'), may hold values from -0.25 to 0.25
- output_weight: bfloat16 [576, 576], P('dp'), may hold values from -3 to 3
- ffn_gain: bfloat16 [576], P('dp'), may hold values from 0.099609375 to 1.8984375
- gate_weight: bfloat16 [576, 1536], P('dp', 'tensor'), may hold values from -0.25 to 0.25
- up_weight: bfloat16 [576, 1536], P('dp', 'tensor'), may hold values from -0.25 to 0.25
- down_weight: bfloat16 [1536, 576], P('tensor', 'dp'), may hold values from -0.15625 to 0.15625
- out_grad: bfloat16 [16, 1024, 576], P('dp', ('context', 'tensor')), may hold values from -6 to 6
Outputs:
- hidden_out: bfloat16 [16, 1024, 576], P('dp', ('context', 'tensor'))
- input_grad: float32 [16, 1024, 576], P('dp', ('context', 'tensor'))
- attn_gain_grad: float32 [576], P('dp')
- query_weight_grad: float32 [576, 576], P('dp')
- key_weight_grad: float32 [576, 192], P('dp')
- value_weight_grad: float32 [576, 192], P('dp')
- output_weight_grad: float32 [576, 576], P('dp')
- ffn_gain_grad: float32 [576], P('dp')
- gate_weight_grad: float32 [576, 1536], P('dp', 'tensor')
- up_weight_grad: float32 [576, 1536], P('dp', 'tensor')
- down_weight_grad: float32 [1536, 576], P('tensor', 'dp')
The draws below stay inside these ranges and needn't reach their ends.
All inputs are finite; a program needn't handle non-finite values.
Results may differ from the reference program's by a relative error of at most 0.024.
Values may be sent and summed in bfloat16 or wider, within the bound.
No kernel may reach another device: no remote copies, remote signals or barrier semaphores. Data moves between devices by JAX's collectives and lax.ppermute only.
A program may use at most 128 MiB of HBM per device.

```python
import math
import jax
import jax.numpy as jnp
from jax import lax

D = 576
HEADS = 9
KV_HEADS = 3
HEAD_DIM = 64
FF = 1536
LEN = 1024
SEQS = 16


def block_scale(rng, extent, shards, low, top_value):
    def one(axis_at, blocks):
        draws = jax.random.uniform(jax.random.fold_in(jax.random.fold_in(rng, 6), axis_at), (blocks,), jnp.float32, low / len(shards), top_value / len(shards))
        return jnp.repeat(jnp.exp(draws), extent[axis_at] // blocks).reshape((-1,) + (1,) * (len(extent) - axis_at - 1))

    level = one(*shards[0])
    for cut in shards[1:]:
        level = level * one(*cut)
    return level


def scatter_about(rng, shape, deviation, reach, pieces=(), held_as=jnp.bfloat16):
    values = jax.random.normal(rng, shape, jnp.float32) * deviation
    if len(pieces) > 0:
        values = block_scale(rng, shape, pieces, -0.22, 0.18) * values
    return jnp.clip(values, min=-reach, max=reach).astype(held_as)


def setup_inputs(seed: int = 0) -> dict:
    splits = jax.random.split(jax.random.key(seed), 12)
    hidden_in = scatter_about(splits[0], (SEQS, LEN, D), 1.0, 6.0, ((0, 2), (1, 16)))
    attn_gain = jnp.clip(1.0 + 0.18 * jax.random.normal(splits[1], (D,), jnp.float32), 0.099609375, 1.8984375).astype(jnp.bfloat16)
    query_weight = scatter_about(splits[2], (D, HEADS * HEAD_DIM), D ** -0.5, 0.25, ((0, 2),))
    key_weight = scatter_about(splits[3], (D, KV_HEADS * HEAD_DIM), D ** -0.5, 0.25, ((0, 2),))
    value_weight = scatter_about(splits[4], (D, KV_HEADS * HEAD_DIM), D ** -0.5, 0.25, ((0, 2),))
    output_weight = scatter_about(splits[5], (HEADS * HEAD_DIM, D), (max(1, D * 8 // LEN)) ** -0.5, 3.0, ((0, 2),))
    ffn_gain = jnp.clip(1.0 + 0.18 * jax.random.normal(splits[6], (D,), jnp.float32), 0.099609375, 1.8984375).astype(jnp.bfloat16)
    gate_weight = scatter_about(splits[7], (D, FF), D ** -0.5, 0.25, ((0, 2), (1, 4)))
    up_weight = scatter_about(splits[8], (D, FF), D ** -0.5, 0.25, ((0, 2), (1, 4)))
    down_weight = scatter_about(splits[9], (FF, D), FF ** -0.5, 0.15625, ((0, 4), (1, 2)))
    out_grad = scatter_about(splits[10], (SEQS, LEN, D), 1.0, 6.0, ((0, 2), (1, 16)))
    return {"hidden_in": hidden_in, "attn_gain": attn_gain, "query_weight": query_weight, "key_weight": key_weight, "value_weight": value_weight, "output_weight": output_weight, "ffn_gain": ffn_gain, "gate_weight": gate_weight, "up_weight": up_weight, "down_weight": down_weight, "out_grad": out_grad}


@jax.custom_vjp
def low(v):
    return lax.optimization_barrier(v.astype(jnp.bfloat16)).astype(jnp.float32)

@jax.custom_vjp
def low_back(v):
    return v

def low_keep(v):
    return (low(v), None)

def low_pass(kept, grad):
    return (grad,)

def back_keep(v):
    return (v, None)

def back_low(kept, grad):
    return (low(grad),)
low.defvjp(low_keep, low_pass)
low_back.defvjp(back_keep, back_low)
EPS = 1e-05
ROPE_BASE = 100000.0
HIGH = lax.Precision.HIGHEST

def rotary(length, half_dim):
    places = jnp.arange(length).astype(jnp.float32)
    frequency = ROPE_BASE ** (-jnp.arange(half_dim).astype(jnp.float32) / half_dim)
    angles = places[:, None] * frequency[None, :]
    return (jnp.cos(angles), jnp.sin(angles))

def rotate(tensor, cosine_table, sine_table):
    half_dim = tensor.shape[-1] // 2
    first_half = tensor[..., :half_dim]
    second_half = tensor[..., half_dim:]
    cosine_b = cosine_table[:, None, :]
    sine_b = sine_table[:, None, :]
    return jnp.concatenate([first_half * cosine_b - second_half * sine_b, second_half * cosine_b + first_half * sine_b], axis=-1)

def attend_block(queries, key_rows, value_rows, start):
    group_count = queries.shape[0]
    row_count = queries.shape[1]
    grouped = queries.reshape(group_count, row_count, KV_HEADS, HEADS // KV_HEADS, HEAD_DIM)
    scores = jnp.einsum('bqgre,bkge->bgrqk', grouped, key_rows, precision=HIGH) * HEAD_DIM ** (-0.5)
    scores = low_back(scores)
    query_place = start + jnp.arange(row_count)
    key_place = jnp.arange(key_rows.shape[1])
    allowed = key_place[None, :] <= query_place[:, None]
    scores = jnp.where(allowed, scores, -1e+30)
    row_max = lax.optimization_barrier(jnp.max(scores, axis=-1, keepdims=True))
    weights = jnp.exp(scores - row_max)
    probability = low(weights / lax.optimization_barrier(jnp.sum(weights, axis=-1, keepdims=True)))
    attended = jnp.einsum('bgrqk,bkge->bqgre', probability, value_rows, precision=HIGH)
    return attended.reshape(group_count, row_count, HEADS * HEAD_DIM)

def block_forward(rows_in, attn_gain, query_weight, key_weight, value_weight, output_weight, ffn_gain, gate_weight, up_weight, down_weight):
    group_count, length, model_width = rows_in.shape
    cosine_table, sine_table = rotary(length, HEAD_DIM // 2)
    inverse = lax.rsqrt(lax.optimization_barrier(jnp.mean(rows_in * rows_in, axis=-1, keepdims=True)) + EPS)
    normed = low(rows_in * inverse * attn_gain)
    queries = jnp.einsum('btd,de->bte', normed, query_weight, precision=HIGH).reshape(group_count, length, HEADS, HEAD_DIM)
    key_rows = jnp.einsum('btd,de->bte', normed, key_weight, precision=HIGH).reshape(group_count, length, KV_HEADS, HEAD_DIM)
    value_rows = jnp.einsum('btd,de->bte', normed, value_weight, precision=HIGH).reshape(group_count, length, KV_HEADS, HEAD_DIM)
    queries = low(rotate(low_back(queries), cosine_table, sine_table))
    key_rows = low(rotate(low_back(key_rows), cosine_table, sine_table))
    value_rows = low(low_back(value_rows))
    block_rows = min(512, length)
    block_count = length // block_rows
    query_blocks = jnp.moveaxis(queries.reshape(group_count, block_count, block_rows, HEADS, HEAD_DIM), 1, 0)
    starts = jnp.arange(block_count) * block_rows

    def one_block(operands):
        return attend_block(operands[0], key_rows, value_rows, operands[1])
    attended = lax.map(jax.checkpoint(one_block), (query_blocks, starts))
    attended = jnp.moveaxis(attended, 0, 1).reshape(group_count, length, HEADS * HEAD_DIM)
    attended = low(low_back(attended))
    middle = rows_in + low_back(jnp.einsum('bte,ed->btd', attended, output_weight, precision=HIGH))
    inverse_two = lax.rsqrt(lax.optimization_barrier(jnp.mean(middle * middle, axis=-1, keepdims=True)) + EPS)
    normed_two = low(middle * inverse_two * ffn_gain)
    gate_act = low_back(jnp.einsum('btd,df->btf', normed_two, gate_weight, precision=HIGH))
    up_act = low_back(jnp.einsum('btd,df->btf', normed_two, up_weight, precision=HIGH))
    hidden_act = low(jax.nn.silu(gate_act) * up_act)
    return middle + low_back(jnp.einsum('btf,fd->btd', hidden_act, down_weight, precision=HIGH))

def reference(hidden_in, attn_gain, query_weight, key_weight, value_weight, output_weight, ffn_gain, gate_weight, up_weight, down_weight, out_grad):
    weights = tuple((weight_arg.astype(jnp.float32) for weight_arg in (attn_gain, query_weight, key_weight, value_weight, output_weight, ffn_gain, gate_weight, up_weight, down_weight)))
    per_step = math.gcd(SEQS, max(1, 4096 // LEN))
    step_count = SEQS // per_step
    inputs = hidden_in.astype(jnp.float32).reshape(step_count, per_step, LEN, D)
    cotangents = out_grad.astype(jnp.float32).reshape(step_count, per_step, LEN, D)

    def one_step(totals, operands):
        rows_in, cotangent = operands
        result, pullback = jax.vjp(block_forward, rows_in, *weights)
        gradients = pullback(cotangent)
        totals = tuple((running + update for running, update in zip(totals, gradients[1:])))
        return (totals, (result, gradients[0]))
    zero_grads = tuple((jnp.zeros(weight_arg.shape, jnp.float32) for weight_arg in weights))
    totals, outputs = lax.scan(one_step, zero_grads, (inputs, cotangents))
    results = outputs[0].reshape(SEQS, LEN, D).astype(jnp.bfloat16)
    input_grads = outputs[1].reshape(SEQS, LEN, D)
    return (results, input_grads, totals[0], totals[1], totals[2], totals[3], totals[4], totals[5], totals[6], totals[7], totals[8])
```

```python
import functools
import jax
import jax.numpy as jnp
from jax import lax
from jax.experimental import pallas as pl
from jax.experimental.pallas import tpu as pltpu
from jax.sharding import PartitionSpec as P

HEADS = 9
KV_HEADS = 3
HEAD_DIM = 64
REPEAT = HEADS // KV_HEADS
QW = HEADS * HEAD_DIM
KW = KV_HEADS * HEAD_DIM
QKW = QW + KW
QKVW = QW + 2 * KW

EPS = 1e-05
ROPE_BASE = 100000.0
F32 = jnp.float32
BF16 = jnp.bfloat16
NEG = -1e30
QB = 128


def nn(left, right):
    return lax.dot_general(left, right, (((1,), (0,)), ((), ())), preferred_element_type=F32)


def nt(left, right):
    return lax.dot_general(left, right, (((1,), (1,)), ((), ())), preferred_element_type=F32)


def tn(left, right):
    return lax.dot_general(left, right, (((0,), (0,)), ((), ())), preferred_element_type=F32)


def swap_halves(tensor):
    width = tensor.shape[-1]
    lane = lax.broadcasted_iota(jnp.int32, tensor.shape, 1)
    ahead = pltpu.roll(tensor, width - HEAD_DIM // 2, 1)
    behind = pltpu.roll(tensor, HEAD_DIM // 2, 1)
    return jnp.where(lane % HEAD_DIM < HEAD_DIM // 2, ahead, behind)


def norm_of(rows):
    inverse = lax.rsqrt(jnp.mean(rows * rows, axis=-1, keepdims=True) + EPS)
    return rows * inverse, inverse


def norm_back(grad_normed, normed, inverse):
    return inverse * (grad_normed - normed * jnp.mean(grad_normed * normed, axis=-1, keepdims=True))


def vmem_call(body, outs, scratch=(), n_smem=0, n_in=0):
    return pl.pallas_call(
        body,
        out_shape=outs,
        in_specs=[pl.BlockSpec(memory_space=pltpu.SMEM)] * n_smem
        + [pl.BlockSpec(memory_space=pltpu.VMEM)] * n_in,
        out_specs=[pl.BlockSpec(memory_space=pltpu.VMEM)] * len(outs),
        scratch_shapes=list(scratch),
    )


def project_body(x_ref, gain_ref, w_ref, cos_ref, sin_ref, q_ref, kv_ref):
    tiles = QKW // cos_ref.shape[1]
    for r in range(0, x_ref.shape[0], QB):
        rows = pl.ds(r, QB)
        normed, _ = norm_of(x_ref[rows, :].astype(F32))
        low = (normed * gain_ref[...]).astype(BF16)
        qkv = nn(low, w_ref[:, :QKVW])
        qk = qkv[:, :QKW]
        cos = jnp.concatenate([cos_ref[rows, :]] * tiles, axis=1)
        sin = jnp.concatenate([sin_ref[rows, :]] * tiles, axis=1)
        turned = (qk * cos + swap_halves(qk) * sin).astype(BF16)
        q_ref[rows, :] = turned[:, :QW]
        kv_ref[rows, :KW] = turned[:, QW:]
        kv_ref[rows, KW:] = qkv[:, QKW:].astype(BF16)


def masks(core):
    shape = (QB, REPEAT * QB)
    key = lax.broadcasted_iota(jnp.int32, shape, 0)
    query = lax.broadcasted_iota(jnp.int32, shape, 1) % QB
    own = key <= query
    other = (key // 32) < (query // 32) + core
    return own, other


def stack_heads(ref, rows, group):
    return jnp.concatenate(
        [
            ref[rows, (group * REPEAT + t) * HEAD_DIM : (group * REPEAT + t + 1) * HEAD_DIM]
            for t in range(REPEAT)
        ],
        axis=0,
    )


def spans(block):
    parts = []
    for side in range(2):
        if block > 0:
            parts.append((side, 0, block * QB, False))
        parts.append((side, block * QB, QB, True))
    return parts


def attend_body(core_ref, q_ref, own_ref, oth_ref, o_ref, l_ref):
    mask = masks(core_ref[0])
    kv_refs = (own_ref, oth_ref)
    for block in range(q_ref.shape[0] // QB):
        rows = pl.ds(block * QB, QB)
        for group in range(KV_HEADS):
            kc = slice(group * HEAD_DIM, (group + 1) * HEAD_DIM)
            vc = slice(KW + group * HEAD_DIM, KW + (group + 1) * HEAD_DIM)
            qs = stack_heads(q_ref, rows, group) * BF16(HEAD_DIM**-0.5)
            scores = []
            for side, start, size, diagonal in spans(block):
                s = nt(kv_refs[side][pl.ds(start, size), kc], qs)
                if diagonal:
                    s = jnp.where(mask[side], s, NEG)
                scores.append(s)
            top = functools.reduce(
                jnp.maximum, [jnp.max(s, axis=0, keepdims=True) for s in scores]
            )
            total = 0.0
            out = 0.0
            for (side, start, size, diagonal), s in zip(spans(block), scores):
                w = jnp.exp(s - top)
                total = total + jnp.sum(w, axis=0, keepdims=True)
                out = out + tn(kv_refs[side][pl.ds(start, size), vc], w.astype(BF16))
            out = (out / total).T
            for t in range(REPEAT):
                head = group * REPEAT + t
                o_ref[rows, head * HEAD_DIM : (head + 1) * HEAD_DIM] = out[
                    t * QB : (t + 1) * QB, :
                ]
            l_ref[block * KV_HEADS + group : block * KV_HEADS + group + 1, :] = top + jnp.log(
                total
            )


def attend_back_body(
    core_ref, q_ref, own_ref, oth_ref, do_ref, o_ref, l_ref, dq_ref, down_ref, doth_ref, acc_ref
):
    mask = masks(core_ref[0])
    kv_refs = (own_ref, oth_ref)
    grads = (down_ref, acc_ref)
    for block in range(q_ref.shape[0] // QB - 1, -1, -1):
        rows = pl.ds(block * QB, QB)
        first = block == q_ref.shape[0] // QB - 1
        for group in range(KV_HEADS):
            kc = slice(group * HEAD_DIM, (group + 1) * HEAD_DIM)
            vc = slice(KW + group * HEAD_DIM, KW + (group + 1) * HEAD_DIM)
            qs = stack_heads(q_ref, rows, group) * BF16(HEAD_DIM**-0.5)
            do = stack_heads(do_ref, rows, group)
            o = stack_heads(o_ref, rows, group)
            delta = jnp.sum((do.astype(F32) * o).T, axis=0, keepdims=True)
            log_sum = l_ref[block * KV_HEADS + group : block * KV_HEADS + group + 1, :]
            dq = 0.0
            for side, start, size, diagonal in spans(block):
                part = pl.ds(start, size)
                key = kv_refs[side][part, kc]
                p = jnp.exp(nt(key, qs) - log_sum)
                if diagonal:
                    p = jnp.where(mask[side], p, 0.0)
                dp = nt(kv_refs[side][part, vc], do)
                ds = (p * (dp - delta)).astype(BF16)
                dv = nn(p.astype(BF16), do)
                dk = nn(ds, qs)
                dq = dq + tn(key, ds)
                if first:
                    grads[side][part, kc] = dk
                    grads[side][part, vc] = dv
                else:
                    grads[side][part, kc] += dk
                    grads[side][part, vc] += dv
            dq = (dq * HEAD_DIM**-0.5).T
            for t in range(REPEAT):
                head = group * REPEAT + t
                dq_ref[rows, head * HEAD_DIM : (head + 1) * HEAD_DIM] = dq[
                    t * QB : (t + 1) * QB, :
                ]
    doth_ref[...] = acc_ref[...].astype(BF16)


def tail_body(
    x_ref,
    gain_ref,
    w_ref,
    cos_ref,
    sin_ref,
    dq_ref,
    dkv_ref,
    recv_ref,
    dmid_ref,
    dx_ref,
    dw_ref,
    dgain_ref,
    low_ref,
    dqkv_ref,
):
    tiles = QKW // cos_ref.shape[1]
    gain_sum = 0.0
    for r in range(0, x_ref.shape[0], QB):
        rows = pl.ds(r, QB)
        normed, inverse = norm_of(x_ref[rows, :].astype(F32))
        low_ref[rows, :] = (normed * gain_ref[...]).astype(BF16)
        dkv = dkv_ref[rows, :] + recv_ref[rows, :].astype(F32)
        dqk = jnp.concatenate([dq_ref[rows, :], dkv[:, :KW]], axis=1)
        cos = jnp.concatenate([cos_ref[rows, :]] * tiles, axis=1)
        sin = jnp.concatenate([sin_ref[rows, :]] * tiles, axis=1)
        dqkv_ref[rows, :QKW] = (dqk * cos - swap_halves(dqk) * sin).astype(BF16)
        dqkv_ref[rows, QKW:] = dkv[:, KW:].astype(BF16)
        da = nt(dqkv_ref[rows, :], w_ref[:, :QKVW])
        gain_sum = gain_sum + jnp.sum(da * normed, axis=0, keepdims=True)
        dx_ref[rows, :] = (
            dmid_ref[rows, :] + norm_back(da * gain_ref[...], normed, inverse)
        ).astype(BF16)
    dgain_ref[...] = jnp.broadcast_to(gain_sum, dgain_ref.shape)
    dw_ref[...] = tn(low_ref[...], dqkv_ref[...]).astype(BF16)


def xor_pairs(count, distance):
    return [(i, i ^ distance) for i in range(count)]


def solution(mesh):
    dp = mesh.shape["dp"]
    ctx = mesh.shape["context"]
    ten = mesh.shape["tensor"]
    chips = ctx // 2

    def swap(value, axis, distance):
        return lax.ppermute(value, axis, xor_pairs(mesh.shape[axis], distance))

    def add_low(left, right):
        return (left.astype(F32) + right.astype(F32)).astype(BF16)

    def pick(value, index, axis=0):
        return lax.dynamic_index_in_dim(value, index, axis, keepdims=False)

    def to_sequences(value, low_rows):
        width = value.shape[-1]
        pieces = value.reshape(chips, ten, 2, low_rows, width).transpose(0, 2, 1, 3, 4)
        moved = lax.all_to_all(
            pieces.reshape(ctx * ten, low_rows, width), ("context", "tensor"), 0, 0, tiled=True
        )
        return moved.reshape(ctx * ten * low_rows, width)

    def to_blocks(value, low_rows):
        width = value.shape[-1]
        moved = lax.all_to_all(
            value.reshape(ctx * ten, low_rows, width), ("context", "tensor"), 0, 0, tiled=True
        )
        moved = moved.reshape(chips, 2, ten, low_rows, width).transpose(0, 2, 1, 3, 4)
        return moved.reshape(chips * ten, 2 * low_rows, width)

    def place_by(pieces_own_first, flag):
        own, other = pieces_own_first
        return jnp.where(flag == 0, jnp.stack([own, other]), jnp.stack([other, own]))

    def gather_attention(pack, ids):
        rows = pack.shape[0]
        if dp == 2:
            half = pick(pack.reshape(2, rows // 2, -1), ids["core"])
            far = swap(half, "dp", 1)
            mine = place_by((half, far), ids["dp"])
        else:
            half = pick(pack.reshape(2, rows // 2, -1), ids["core"])
            mine = lax.all_gather(half, "dp", axis=0, tiled=False)
        theirs = swap(mine, "context", 1)
        both = place_by((mine, theirs), ids["core"])
        return both.transpose(1, 0, 2, 3).reshape(dp, rows, -1)

    def gather_ffn(pack, ids):
        rows, cols = pack.shape
        quarter = pick(pack.reshape(ctx, rows // ctx, cols), ids["context"])
        strip = jnp.concatenate(
            [quarter] + [swap(quarter, "tensor", d) for d in range(1, ten)], axis=1
        )
        if dp == 2:
            half = rows // ctx // 2
            from_x = swap(strip, "dp", 1)
            from_y = swap(strip, "context", 2)
            corner = jnp.concatenate(
                [swap(from_x[:half], "context", 2), swap(from_y[half:], "dp", 1)], axis=0
            )
            mine = jnp.stack([jnp.stack([strip, from_y]), jnp.stack([from_x, corner])])
        else:
            from_y = swap(strip, "context", 2)
            mine = jnp.stack([strip, from_y])
            mine = lax.all_gather(mine, "dp", axis=0, tiled=False)
        theirs = swap(mine, "context", 1)
        whole = jnp.zeros((dp, ctx, rows // ctx, ten * cols), BF16)
        for x in range(dp):
            x_at = (ids["dp"] ^ x) if dp == 2 else x
            for y in range(chips):
                for c, source in enumerate((mine, theirs)):
                    q_at = ids["context"] ^ (2 * y + c)
                    whole = lax.dynamic_update_slice(
                        whole, source[x, y][None, None], (x_at, q_at, 0, 0)
                    )
        return whole.reshape(dp, rows, ten * cols)

    def reduce_pack(grads, ids, relative):
        rows, width = grads.shape[1:]
        quarter = rows // ctx
        cols = width // ten
        view = grads.reshape(dp, chips, 2, quarter, width)
        mine = pick(view, ids["core"], 2)
        got = swap(pick(view, 1 - ids["core"], 2), "context", 1)
        mine = add_low(mine, got)
        y_own, y_far = ids["context"] // 2, 1 - ids["context"] // 2
        if dp == 2:
            half = quarter // 2
            x_own, x_far = ids["dp"], 1 - ids["dp"]
            near, far = pick(mine, x_own), pick(mine, x_far)
            upper = add_low(near[:, :half], swap(far[:, :half], "dp", 1))
            side, away = pick(mine, y_own, 1), pick(mine, y_far, 1)
            lower = add_low(side[:, half:], swap(away[:, half:], "context", 2))
            upper = add_low(pick(upper, y_own), swap(pick(upper, y_far), "context", 2))
            lower = add_low(pick(lower, x_own), swap(pick(lower, x_far), "dp", 1))
            strip = jnp.concatenate([upper, lower], axis=0)
        else:
            mine = lax.psum_scatter(mine, "dp", scatter_dimension=0, tiled=False)
            strip = add_low(pick(mine, y_own), swap(pick(mine, y_far), "context", 2))
        strip = strip.reshape(quarter, ten, cols).transpose(1, 0, 2)
        total = pick(strip, 0 if relative else ids["tensor"]).astype(F32)
        for d in range(1, ten):
            chunk = pick(strip, d if relative else ids["tensor"] ^ d)
            total = total + swap(chunk, "tensor", d).astype(F32)
        piece = total.astype(BF16)
        if not relative:
            spread = jnp.zeros((ten, quarter, cols), BF16)
            for d in range(ten):
                part = piece if d == 0 else swap(piece, "tensor", d)
                spread = lax.dynamic_update_slice(spread, part[None], (ids["tensor"] ^ d, 0, 0))
            piece = spread.transpose(1, 0, 2).reshape(quarter, width)
        pair = place_by((piece, swap(piece, "context", 2)), ids["context"] // 2)
        whole = place_by((pair, swap(pair, "context", 1)), ids["core"])
        return whole.transpose(1, 0, 2, 3).reshape(rows, -1).astype(F32)

    def body(
        hidden_in,
        attn_gain,
        query_weight,
        key_weight,
        value_weight,
        output_weight,
        ffn_gain,
        gate_weight,
        up_weight,
        down_weight,
        out_grad,
    ):
        seq_count, local_len, width = hidden_in.shape
        part = attn_gain.shape[0]
        low_rows = local_len // 2
        tokens = ctx * ten * low_rows
        ff_part = gate_weight.shape[1]
        ids = {
            "dp": lax.axis_index("dp"),
            "context": lax.axis_index("context"),
            "tensor": lax.axis_index("tensor"),
        }
        ids["core"] = ids["context"] % 2
        core = ids["core"].reshape(1).astype(jnp.int32)

        attn_rows = -(-(part + 1) // 64) * 64
        ffn_rows = -(-(3 * part) // 64) * 64
        attn_width = QKVW + width
        gains = jnp.concatenate([attn_gain, ffn_gain, jnp.zeros((attn_width - 2 * part,), BF16)])
        attn_pack = jnp.concatenate(
            [
                jnp.concatenate([query_weight, key_weight, value_weight, output_weight], axis=1),
                gains[None],
                jnp.zeros((attn_rows - part - 1, attn_width), BF16),
            ],
            axis=0,
        )
        ffn_pack = jnp.concatenate(
            [
                gate_weight,
                up_weight,
                down_weight.T,
                jnp.zeros((ffn_rows - 3 * part, ff_part), BF16),
            ],
            axis=0,
        )
        attn_all = gather_attention(attn_pack, ids)
        ffn_all = gather_ffn(ffn_pack, ids)
        w_attn = attn_all[:, :part].reshape(width, attn_width)
        gain_one = attn_all[:, part, :part].reshape(1, width).astype(F32)
        gain_two = attn_all[:, part, part : 2 * part].reshape(1, width).astype(F32)
        out_all = w_attn[:, QKVW:]
        gate_all = ffn_all[:, :part].reshape(width, ten * ff_part)
        up_all = ffn_all[:, part : 2 * part].reshape(width, ten * ff_part)
        down_all = ffn_all[:, 2 * part : 3 * part].reshape(width, ten * ff_part)

        row = jnp.arange(tokens, dtype=jnp.int32)
        places = 2 * low_rows * (row // low_rows) + low_rows * ids["core"] + row % low_rows
        lane = jnp.arange(2 * HEAD_DIM, dtype=jnp.int32)
        frequency = ROPE_BASE ** (
            -(lane % (HEAD_DIM // 2)).astype(F32) / (HEAD_DIM // 2)
        )
        angles = places.astype(F32)[:, None] * frequency[None, :]
        cos = jnp.cos(angles)
        sin = jnp.where(lane % HEAD_DIM < HEAD_DIM // 2, -1.0, 1.0)[None, :] * jnp.sin(angles)

        x = to_sequences(hidden_in, low_rows)
        dy = to_sequences(out_grad, low_rows)

        q, kv = vmem_call(
            project_body,
            [
                jax.ShapeDtypeStruct((tokens, QW), BF16),
                jax.ShapeDtypeStruct((tokens, 2 * KW), BF16),
            ],
            n_in=5,
        )(x, gain_one, w_attn, cos, sin)
        kv_far = swap(kv, "context", 1)
        blocks = tokens // QB
        attended, log_sums = vmem_call(
            attend_body,
            [
                jax.ShapeDtypeStruct((tokens, QW), F32),
                jax.ShapeDtypeStruct((blocks * KV_HEADS, REPEAT * QB), F32),
            ],
            n_smem=1,
            n_in=3,
        )(core, q, kv, kv_far)

        rows_in = x.astype(F32)
        attended_low = attended.astype(BF16)
        middle = rows_in + nn(attended_low, out_all)
        normed_two, inverse_two = norm_of(middle)
        c = (normed_two * gain_two).astype(BF16)
        gate_act = nn(c, gate_all)
        up_act = nn(c, up_all)
        sigmoid = jax.nn.sigmoid(gate_act)
        silu = gate_act * sigmoid
        hidden = (silu * up_act).astype(BF16)
        hidden_out = (middle + nt(hidden, down_all)).astype(BF16)
        grad_hidden = nn(dy, down_all)
        d_up = (grad_hidden * silu).astype(BF16)
        d_gate = (grad_hidden * up_act * (sigmoid * (1.0 + gate_act * (1.0 - sigmoid)))).astype(
            BF16
        )
        down_grad = tn(dy, hidden)
        gate_grad = tn(c, d_gate)
        up_grad = tn(c, d_up)
        dc = nt(d_gate, gate_all) + nt(d_up, up_all)
        ffn_gain_term = jnp.sum(dc * normed_two, axis=0)
        d_middle = dy.astype(F32) + norm_back(dc * gain_two, normed_two, inverse_two)
        d_mid_low = d_middle.astype(BF16)
        out_grad_w = tn(attended_low, d_mid_low)
        d_attended = nt(d_mid_low, out_all).astype(BF16)

        ffn_grads = jnp.concatenate(
            [
                gate_grad.astype(BF16).reshape(dp, part, -1),
                up_grad.astype(BF16).reshape(dp, part, -1),
                down_grad.astype(BF16).reshape(dp, part, -1),
                jnp.zeros((dp, ffn_rows - 3 * part, ten * ff_part), BF16),
            ],
            axis=1,
        )
        ffn_sum = reduce_pack(ffn_grads, ids, True)

        dq, dkv, dkv_far = vmem_call(
            attend_back_body,
            [
                jax.ShapeDtypeStruct((tokens, QW), F32),
                jax.ShapeDtypeStruct((tokens, 2 * KW), F32),
                jax.ShapeDtypeStruct((tokens, 2 * KW), BF16),
            ],
            scratch=[pltpu.VMEM((tokens, 2 * KW), F32)],
            n_smem=1,
            n_in=6,
        )(core, q, kv, kv_far, d_attended, attended, log_sums)
        dkv_back = swap(dkv_far, "context", 1)
        dx, qkv_grad, gain_term = vmem_call(
            tail_body,
            [
                jax.ShapeDtypeStruct((tokens, width), BF16),
                jax.ShapeDtypeStruct((width, QKVW), BF16),
                jax.ShapeDtypeStruct((8, width), F32),
            ],
            scratch=[
                pltpu.VMEM((tokens, width), BF16),
                pltpu.VMEM((tokens, QKVW), BF16),
            ],
            n_in=9,
        )(x, gain_one, w_attn, cos, sin, dq, dkv, dkv_back, d_middle)

        gain_rows = jnp.concatenate(
            [
                gain_term[0].astype(BF16).reshape(dp, 1, part),
                ffn_gain_term.astype(BF16).reshape(dp, 1, part),
                jnp.zeros((dp, 1, attn_width - 2 * part), BF16),
            ],
            axis=2,
        )
        attn_grads = jnp.concatenate(
            [
                jnp.concatenate([qkv_grad, out_grad_w.astype(BF16)], axis=1).reshape(
                    dp, part, attn_width
                ),
                gain_rows,
                jnp.zeros((dp, attn_rows - part - 1, attn_width), BF16),
            ],
            axis=1,
        )
        attn_sum = reduce_pack(attn_grads, ids, False)

        out_blocks = to_blocks(hidden_out, low_rows)
        in_blocks = to_blocks(dx, low_rows).astype(F32)
        return (
            out_blocks,
            in_blocks,
            attn_sum[part, :part],
            attn_sum[:part, :QW],
            attn_sum[:part, QW:QKW],
            attn_sum[:part, QKW:QKVW],
            attn_sum[:part, QKVW:],
            attn_sum[part, part : 2 * part],
            ffn_sum[:part],
            ffn_sum[part : 2 * part],
            ffn_sum[2 * part : 3 * part].T,
        )

    weight_rows = P("dp", None)
    tokens_spec = P("dp", ("context", "tensor"), None)
    return jax.shard_map(
        body,
        mesh=mesh,
        in_specs=(
            tokens_spec,
            P("dp"),
            weight_rows,
            weight_rows,
            weight_rows,
            weight_rows,
            P("dp"),
            P("dp", "tensor"),
            P("dp", "tensor"),
            P("tensor", "dp"),
            tokens_spec,
        ),
        out_specs=(
            tokens_spec,
            tokens_spec,
            P("dp"),
            weight_rows,
            weight_rows,
            weight_rows,
            weight_rows,
            P("dp"),
            P("dp", "tensor"),
            P("dp", "tensor"),
            P("tensor", "dp"),
        ),
        check_vma=False,
    )
```
